512 devices in a mesh: box: 128 (over z, y, core), coarse: 4 (over x).
Axes of the slice: x: 4, y: 8, z: 8, core: 2. Of those that a mesh axis runs over, the one named last changes fastest.
Arguments:
- points: float32 [128, 8, 3, 256], P('box', 'coarse'), may hold values from 0 to 1
- self_gain: float32 [128, 8, 256], P('box', 'coarse'), may hold values from 1.5 to 4
- pivots: int32 [128, 8, 256], P('box', 'coarse'), may hold values from 0 to 255, each once within a row
- interp: float32 [128, 8, 128, 128], P('box', 'coarse'), may hold values from -0.5 to 0.5
- neighbors: int32 [128, 8, 6], P('box', 'coarse'), may hold values from 0 to 15, as said below
- rhs: float32 [128, 8, 256, 512], P('box', 'coarse'), may hold values from -6 to 6
Outputs:
- solution: float32 [128, 8, 256, 512], P('box', 'coarse')
The draws below stay inside these ranges and needn't reach their ends.
Inputs may be any that keep to these rules, and one draw needn't show every extreme that they name: `pivots`: each box's row orders all 256 of its points once; the first 128 form its skeleton. `neighbors`: each box lists 6 different boxes; n < 8 names child n of the previous parent, 8 + n child n of the next parent.
All inputs are finite; a program needn't handle non-finite values.
Results may differ from the reference program's by a relative error of at most 0.0003.
Values sent between devices are 32-bit elements; how exact they have to be, the bound alone decides.
No kernel may reach another device: no remote copies, remote signals or barrier semaphores. Data moves between devices by JAX's collectives and lax.ppermute only.
A program may use at most 64 MiB of HBM per device.

```python
import math
import jax
import jax.numpy as jnp
from jax import lax

NP = 256
K = 128
R = 128
COLS = 512
CHILD = 8
NB = 6
GROUPS = 128


def draw_neighbors(key, part):
    keys = jax.random.split(key, GROUPS * CHILD)
    rows = jax.vmap(lambda single: jax.random.permutation(single, 2 * CHILD)[:NB])(keys)
    return rows.reshape(GROUPS, CHILD, NB).astype(jnp.int32)


def block_levels(stream_key, extent, cuts, low, top_value):
    def one(dim, parts):
        steps = jax.random.uniform(jax.random.fold_in(jax.random.fold_in(stream_key, 6), dim), (parts,), jnp.float32, low / len(cuts), top_value / len(cuts))
        return jnp.repeat(jnp.exp(steps), extent[dim] // parts).reshape((-1,) + (1,) * (len(extent) - dim - 1))

    gain = one(*cuts[0])
    for cut in cuts[1:]:
        gain = gain * one(*cut)
    return gain


def noise(own_key, shape, spread, bound, cuts=(), kind=jnp.bfloat16):
    loudness = block_levels(own_key, shape, cuts, -0.22, 0.18) if cuts else 1.0
    drawn = jax.random.normal(own_key, shape, jnp.float32) * spread * loudness
    return jnp.minimum(jnp.maximum(drawn, -bound), bound).astype(kind)


def setup_inputs(seed: int = 0) -> dict:
    splits = jax.random.split(jax.random.key(seed), 7)
    points = jnp.clip(1.0 * jax.random.uniform(splits[0], (GROUPS, CHILD, 3, NP), jnp.float32) ** block_levels(splits[0], (GROUPS, CHILD, 3, NP), ((0, 128), (1, 4)), -0.2, 0.2), 0.0, 1.0)
    self_gain = jnp.clip(jnp.exp(math.log(4.0) - 0.98082925 * jax.random.uniform(splits[1], (GROUPS, CHILD, NP), jnp.float32) ** block_levels(splits[1], (GROUPS, CHILD, NP), ((0, 128), (1, 4)), -0.2, 0.2)), 1.5, 4.0)
    pivots = jax.vmap(lambda own: jax.random.permutation(own, NP))(jax.random.split(splits[2], GROUPS * CHILD)).reshape((GROUPS, CHILD, NP)).astype(jnp.int32)
    interp = noise(splits[3], (GROUPS, CHILD, K, R), R ** -0.5, 0.5, ((0, 128), (1, 4)), jnp.float32)
    neighbors = draw_neighbors(jax.random.fold_in(splits[6], 71), 0)
    rhs = noise(splits[5], (GROUPS, CHILD, NP, COLS), 1.0, 6.0, ((0, 128), (1, 4)), jnp.float32)
    return dict(points=points, self_gain=self_gain, pivots=pivots, interp=interp, neighbors=neighbors, rhs=rhs)


softening = 0.0025

def kernel_block(targets, sources):
    difference = targets[:, :, None] - sources[:, None, :]
    return lax.rsqrt(lax.optimization_barrier(jnp.sum(difference * difference, axis=0)) + softening)

def product(left, right):
    return jnp.dot(left, right, precision=lax.Precision.HIGHEST)

def chol_apply(factor, right):
    return jax.scipy.linalg.cho_solve((factor, True), right)

def box_corners(group_ids, child_ids):
    along_x = 2 * group_ids + child_ids % 2
    along_y = child_ids // 2 % 2
    along_z = child_ids // 4
    return jnp.stack([along_x, along_y, along_z], axis=-1).astype(jnp.float32)

def factor_box(located, gains, order, interp, right_side):
    ordered = jnp.take(located, order, axis=1)
    ordered_gain = jnp.take(gains, order, axis=0)
    ordered_rhs = jnp.take(right_side, order, axis=0)
    kernel = kernel_block(ordered, ordered)
    count = ordered.shape[1]
    rank = interp.shape[0]
    matrix = (kernel + jnp.diag(ordered_gain * lax.optimization_barrier(jnp.sum(kernel, axis=1)))) / count
    skel_skel = matrix[:rank, :rank]
    skel_red = matrix[:rank, rank:]
    red_skel = matrix[rank:, :rank]
    red_red = matrix[rank:, rank:]
    shifted = product(interp.T, skel_skel)
    red_block = red_red - product(interp.T, skel_red) - product(red_skel, interp) + product(shifted, interp)
    cross = red_skel - shifted
    red_factor = jnp.linalg.cholesky(red_block)
    coupling = chol_apply(red_factor, cross)
    schur = skel_skel - product(cross.T, coupling)
    reduced = ordered_rhs[rank:] - product(interp.T, ordered_rhs[:rank])
    interior = chol_apply(red_factor, reduced)
    skeleton_rhs = ordered_rhs[:rank] - product(coupling.T, reduced)
    schur_factor = jnp.linalg.cholesky(schur)
    local_solve = chol_apply(schur_factor, skeleton_rhs)
    return (schur_factor, coupling, interior, local_solve, ordered[:, :rank])

def coarse_weights(neighbor_rows, own_child):
    listed = jnp.any(neighbor_rows[:, :, None] == jnp.arange(2 * CHILD, dtype=jnp.int32)[None, None, :], axis=1).astype(jnp.float32)
    siblings = (own_child[:, None] != jnp.arange(CHILD, dtype=jnp.int32)[None, :]).astype(jnp.float32)
    return jnp.concatenate([listed[:, :CHILD], siblings, listed[:, CHILD:]], axis=1)

def coarse_terms(skeleton, cand_pts, cand_rhs, weights):
    blocks = jax.vmap(lambda target: jax.vmap(lambda source: kernel_block(target, source))(cand_pts))(skeleton)
    return jnp.einsum('bckl,cln->bkn', blocks * weights[:, :, None, None], cand_rhs, precision=lax.Precision.HIGHEST) / NP

def finish_box(schur_factor, coupling, interior, local_solve, correction, interp, order):
    coarse = local_solve - chol_apply(schur_factor, correction)
    redundant = interior - product(coupling, coarse)
    skeletal = coarse - product(interp, redundant)
    ordered = jnp.concatenate([skeletal, redundant], axis=0)
    return jnp.zeros_like(ordered).at[order].set(ordered)

def reference(points, self_gain, pivots, interp, neighbors, rhs):
    group_ids = jnp.arange(GROUPS, dtype=jnp.int32)[:, None] + jnp.zeros((1, CHILD), jnp.int32)
    child_ids = jnp.zeros((GROUPS, 1), jnp.int32) + jnp.arange(CHILD, dtype=jnp.int32)[None, :]
    located = points + box_corners(group_ids, child_ids)[..., None]
    schur_factor, coupling, interior, local_solve, skeleton = lax.map(lambda items: jax.vmap(factor_box)(*items), (located, self_gain, pivots, interp, rhs))
    padded_rhs = jnp.pad(local_solve, ((1, 1), (0, 0), (0, 0), (0, 0)))
    padded_pts = jnp.pad(skeleton, ((1, 1), (0, 0), (0, 0), (0, 0)))
    own_child = jnp.arange(CHILD, dtype=jnp.int32)

    def per_group(items):
        index, schur_g, coupling_g, interior_g, solve_g, skeleton_g, interp_g, pivots_g, neighbors_g = items
        cand_rhs = lax.dynamic_slice_in_dim(padded_rhs, index, 3, 0).reshape(3 * CHILD, K, COLS)
        cand_pts = lax.dynamic_slice_in_dim(padded_pts, index, 3, 0).reshape(3 * CHILD, 3, K)
        weights = coarse_weights(neighbors_g, own_child)
        correction = coarse_terms(skeleton_g, cand_pts, cand_rhs, weights)
        return jax.vmap(finish_box)(schur_g, coupling_g, interior_g, solve_g, correction, interp_g, pivots_g)
    return lax.map(per_group, (jnp.arange(GROUPS, dtype=jnp.int32), schur_factor, coupling, interior, local_solve, skeleton, interp, pivots, neighbors))
```

```python
import jax
import jax.numpy as jnp
from jax import lax
from jax.experimental import pallas as pl
from jax.experimental.pallas import tpu as pltpu
from jax.sharding import PartitionSpec as P

NP = 256
K = 128
COLS = 512
CHILD = 8
NB = 6
HERE = 2
PANELS = COLS // 128
ROWS = PANELS * K + 8
TARGETS = 3 * HERE
F32 = jnp.float32
BF16 = jnp.bfloat16

softening = 0.0025

NN = (((1,), (0,)), ((), ()))
NT = (((1,), (1,)), ((), ()))
TN = (((0,), (0,)), ((), ()))


def pieces(x):
    high = x.astype(BF16)
    return high, (x - high.astype(F32)).astype(BF16)


def multiply(left, right, dims=NN):
    dot = lambda a, b: lax.dot_general(a, b, dims, preferred_element_type=F32)
    return dot(left[0], right[0]) + (dot(left[0], right[1]) + dot(left[1], right[0]))


def select(x, chosen, dims):
    dot = lambda a: lax.dot_general(a, chosen, dims, preferred_element_type=F32)
    high, rest = x.astype(BF16), None
    rest = x - high.astype(F32)
    mid = rest.astype(BF16)
    low = (rest - mid.astype(F32)).astype(BF16)
    return dot(high) + (dot(mid) + dot(low))


def kernel_block(columns, rows):
    square = None
    for axis in range(3):
        difference = columns[axis] - rows[axis]
        square = difference * difference if square is None else square + difference * difference
    return lax.rsqrt(square + softening)


def as_columns(rows8):
    turned = jnp.transpose(rows8)
    return [turned[:, axis : axis + 1] for axis in range(3)]


def factor_kernel(neighbors, points, gain, pivots, interp, rhs, message, info, inverse, response):
    group = lax.axis_index("box")
    even = (group % 2) == 0
    first_child = HERE * lax.axis_index("coarse")
    sub = lax.broadcasted_iota(jnp.int32, (NP, NP), 0)
    lane = lax.broadcasted_iota(jnp.int32, (NP, NP), 1)
    small_sub = lax.broadcasted_iota(jnp.int32, (8, NP), 0)
    small_lane = lax.broadcasted_iota(jnp.int32, (1, 128), 1)
    for box in range(HERE):
        child = first_child + box
        corner = (2 * group + child % 2, child // 2 % 2, child // 4)
        rows8 = jnp.zeros((8, NP), F32)
        for axis in range(3):
            coordinate = points[box, axis : axis + 1, :] + corner[axis].astype(F32)
            rows8 = jnp.where(small_sub == axis, coordinate, rows8)
        columns = as_columns(rows8)
        kernel = kernel_block(columns, [rows8[axis : axis + 1] for axis in range(3)])
        row_sum = jnp.sum(kernel, axis=0, keepdims=True)
        row_scale = lax.rsqrt(gain[box : box + 1, :] * row_sum)
        column_scale = jnp.transpose(jnp.broadcast_to(row_scale, (8, NP)))[:, :1]
        diagonal = sub == lane
        residual = jnp.where(diagonal, 0.25, 0.0) - 0.75 * (column_scale * kernel * row_scale)
        r = pieces(residual)
        square = multiply(r, r)
        w = (32.0 / 31.0) * square - jnp.where(diagonal, 1.0 / 31.0, 0.0)
        wp = pieces(w)
        v = (961.0 * 2.0 / 1921.0) * multiply(wp, wp) - jnp.where(diagonal, 1.0 / 1921.0, 0.0)
        tail = w + v + multiply(wp, pieces(v))
        series = residual + tail + multiply(r, pieces(tail))
        factor = 0.75 * NP * (32.0 / 31.0) * (1922.0 / 1921.0)
        scaled = (factor * column_scale) * (series + jnp.where(diagonal, 1.0, 0.0)) * row_scale
        inverse[box] = scaled
        chosen = jnp.where(sub == pivots[box : box + 1, :], 1.0, 0.0).astype(BF16)
        keep = chosen[:, :K].astype(F32)
        lifted = keep + select_right(chosen[:, K:], interp[box])
        lifted_pieces = pieces(lifted)
        answer = multiply(pieces(scaled), lifted_pieces)
        response[box] = answer
        solved = multiply(pieces(answer), pieces(rhs[box]), TN)
        for panel in range(PANELS):
            message[box, panel * K : (panel + 1) * K, :] = solved[:, panel * 128 : (panel + 1) * 128]
        skeleton = select(rows8, chosen[:, :K], NN)
        previous = jnp.zeros((1, 128), jnp.bool_)
        following = jnp.zeros((1, 128), jnp.bool_)
        for slot in range(NB):
            listed = neighbors[box, slot]
            previous = previous | (small_lane == listed)
            following = following | (small_lane == listed - CHILD)
        previous = jnp.where(previous, 1.0, 0.0)
        following = jnp.where(following, 1.0, 0.0)
        for_inner = jnp.where(even, following, previous)
        for_outer = jnp.where(even, previous, following)
        rows = lax.broadcasted_iota(jnp.int32, (8, 128), 0)
        packed = jnp.where(rows == 3, for_inner, jnp.where(rows == 4, for_outer, skeleton))
        message[box, PANELS * K :, :] = packed
        info[box] = packed


def select_right(chosen, x):
    dot = lambda a: lax.dot_general(chosen, a, NT, preferred_element_type=F32)
    high = x.astype(BF16)
    rest = x - high.astype(F32)
    mid = rest.astype(BF16)
    low = (rest - mid.astype(F32)).astype(BF16)
    return dot(high) + (dot(mid) + dot(low))


VMEM = pl.BlockSpec(memory_space=pltpu.VMEM)
SMEM = pl.BlockSpec(memory_space=pltpu.SMEM)


def shape(*dims):
    return jax.ShapeDtypeStruct(dims, F32)


def factor_boxes(neighbors, points, gain, pivots, interp, rhs):
    return pl.pallas_call(
        factor_kernel,
        out_shape=(
            shape(HERE, ROWS, 128),
            shape(HERE, 8, 128),
            shape(HERE, NP, NP),
            shape(HERE, NP, K),
        ),
        in_specs=[SMEM] + [VMEM] * 5,
        out_specs=(VMEM,) * 4,
        name="factor_boxes",
    )(neighbors, points, gain, pivots, interp, rhs)


def apply_kernel(inverse, rhs, start):
    for box in range(HERE):
        start[box] = multiply(pieces(inverse[box]), pieces(rhs[box]))


def apply_inverse(inverse, rhs):
    return pl.pallas_call(
        apply_kernel,
        out_shape=shape(HERE, NP, COLS),
        in_specs=[VMEM] * 2,
        out_specs=VMEM,
        name="apply_inverse",
    )(inverse, rhs)


def terms_kernel(steps, *refs):
    sources = refs[: len(steps)]
    own, inner, outer = refs[len(steps) : len(steps) + 3]
    before = refs[len(steps) + 3] if len(refs) == len(steps) + 5 else None
    total = refs[-1]
    place = lax.axis_index("coarse")
    lane = lax.broadcasted_iota(jnp.int32, (1, 128), 1)
    targets = []
    for kind, ref in enumerate((own, inner, outer)):
        for box in range(HERE):
            targets.append((kind, box, as_columns(ref[box]), ref))
    right = []
    for ref in sources:
        values = [
            jnp.concatenate([ref[j, p * K : (p + 1) * K, :] for p in range(PANELS)], axis=1)
            for j in range(HERE)
        ]
        right.append(pieces(jnp.concatenate(values, axis=0)))
    for kind, box, columns, ref in targets:
        result = before[kind * HERE + box] if before is not None else None
        for step, source, values in zip(steps, sources, right):
            blocks = []
            for j in range(HERE):
                if kind == 0 and step == 0 and j == box:
                    blocks.append(jnp.zeros((K, K), F32))
                    continue
                child = HERE * (place ^ step) + j
                rows = [source[j, PANELS * K + axis : PANELS * K + axis + 1, :] for axis in range(3)]
                block = kernel_block(columns, rows)
                if kind == 0:
                    block = block * (1.0 / NP)
                else:
                    row = ref[box, 2 + kind : 3 + kind, :]
                    weight = jnp.sum(jnp.where(lane == child, row, 0.0), axis=1, keepdims=True)
                    block = block * (weight * (1.0 / NP))
                blocks.append(block)
            term = multiply(pieces(jnp.concatenate(blocks, axis=1)), values)
            result = term if result is None else result + term
        total[kind * HERE + box] = result


def coarse_terms(steps, sources, infos, before=None):
    operands = [*sources, *infos] + ([] if before is None else [before])

    def body(*refs):
        terms_kernel(steps, *refs)

    return pl.pallas_call(
        body,
        out_shape=shape(TARGETS, K, COLS),
        in_specs=[VMEM] * len(operands),
        out_specs=VMEM,
        name="coarse_terms_" + "_".join(str(step) for step in steps),
    )(*operands)


def finish_kernel(start, response, total, inner, outer, out):
    for box in range(HERE):
        correction = total[box] + (inner[box] + outer[box])
        out[box] = start[box] - multiply(pieces(response[box]), pieces(correction))


def finish_boxes(start, response, total, inner, outer):
    return pl.pallas_call(
        finish_kernel,
        out_shape=shape(HERE, NP, COLS),
        in_specs=[VMEM] * 5,
        out_specs=VMEM,
        name="finish_boxes",
    )(start, response, total, inner, outer)


def exchanged(block, axis, partner):
    devices = range(lax.axis_size(axis))
    return lax.ppermute(block, axis, [(i, partner(i)) for i in devices if partner(i) in devices])


def inner_partner(i):
    return i ^ 1


def outer_partner(i):
    return i - 1 if i % 2 == 0 else i + 1


def per_device(points, self_gain, pivots, interp, neighbors, rhs):
    message, info, inverse, response = factor_boxes(
        neighbors[0], points[0], self_gain[0], pivots[0], interp[0], rhs[0]
    )
    from_1 = exchanged(message, "coarse", lambda i: i ^ 1)
    from_3 = exchanged(message, "coarse", lambda i: i ^ 3)
    from_2 = exchanged(message, "coarse", lambda i: i ^ 2)
    outer_info = exchanged(info, "box", outer_partner)
    inner_info = exchanged(info, "box", inner_partner)
    start = apply_inverse(inverse, rhs[0])
    infos = (info, inner_info, outer_info)
    total = coarse_terms((0,), (message,), infos)
    total = coarse_terms((1, 3), (from_1, from_3), infos, total)
    total = coarse_terms((2,), (from_2,), infos, total)
    outer = exchanged(total[2 * HERE :], "box", outer_partner)
    inner = exchanged(total[HERE : 2 * HERE], "box", inner_partner)
    return finish_boxes(start, response, total[:HERE], inner, outer)[None]


def solution(mesh):
    in_specs = (
        P("box", "coarse", None, None),
        P("box", "coarse", None),
        P("box", "coarse", None),
        P("box", "coarse", None, None),
        P("box", "coarse", None),
        P("box", "coarse", None, None),
    )
    out_specs = P("box", "coarse", None, None)
    return jax.shard_map(
        per_device, mesh=mesh, in_specs=in_specs, out_specs=out_specs, check_vma=False
    )
```

```python
import jax
import jax.numpy as jnp
from jax import lax
from jax.experimental import pallas as pl
from jax.experimental.pallas import tpu as pltpu
from jax.sharding import PartitionSpec as P

NP = 256
K = 128
COLS = 512
CHILD = 8
NB = 6
HERE = 2
PANELS = COLS // 128
ROWS = K + 8
F32 = jnp.float32
BF16 = jnp.bfloat16

softening = 0.0025

GRANT = pltpu.CompilerParams(vmem_limit_bytes=16 * 2**20)

NN = (((1,), (0,)), ((), ()))
NT = (((1,), (1,)), ((), ()))
TN = (((0,), (0,)), ((), ()))


def pieces(x):
    high = x.astype(BF16)
    return high, (x - high.astype(F32)).astype(BF16)


def multiply(left, right, dims=NN):
    dot = lambda a, b: lax.dot_general(a, b, dims, preferred_element_type=F32)
    return dot(left[0], right[0]) + (dot(left[0], right[1]) + dot(left[1], right[0]))


def select(x, chosen, dims):
    dot = lambda a: lax.dot_general(a, chosen, dims, preferred_element_type=F32)
    high, rest = x.astype(BF16), None
    rest = x - high.astype(F32)
    mid = rest.astype(BF16)
    low = (rest - mid.astype(F32)).astype(BF16)
    return dot(high) + (dot(mid) + dot(low))


def kernel_block(columns, rows):
    square = None
    for axis in range(3):
        difference = columns[axis] - rows[axis]
        square = difference * difference if square is None else square + difference * difference
    return lax.rsqrt(square + softening)


def as_columns(rows8):
    turned = jnp.transpose(rows8)
    return [turned[:, axis : axis + 1] for axis in range(3)]


def factor_kernel(
    neighbors, points, gain, pivots, interp_hbm, rhs_hbm,
    message, inverse, response, rhs, interp, sems,
):
    loads = [
        (
            pltpu.make_async_copy(interp_hbm.at[box], interp.at[box], sems.at[0, box]),
            pltpu.make_async_copy(rhs_hbm.at[box], rhs.at[box], sems.at[1, box]),
        )
        for box in range(HERE)
    ]
    for step in range(2):
        for box in range(HERE):
            loads[box][step].start()
    group = lax.axis_index("box")
    first_child = HERE * lax.axis_index("coarse")
    sub = lax.broadcasted_iota(jnp.int32, (NP, NP), 0)
    lane = lax.broadcasted_iota(jnp.int32, (NP, NP), 1)
    small_sub = lax.broadcasted_iota(jnp.int32, (8, NP), 0)
    info_sub = lax.broadcasted_iota(jnp.int32, (8, 128), 0)
    info_lane = lax.broadcasted_iota(jnp.int32, (8, 128), 1)
    diagonal = sub == lane

    def stages(box):
        child = first_child + box
        corner = (2 * group + child % 2, child // 2 % 2, child // 4)
        rows8 = jnp.zeros((8, NP), F32)
        for axis in range(3):
            coordinate = points[axis, box : box + 1, :] + corner[axis].astype(F32)
            rows8 = jnp.where(small_sub == axis, coordinate, rows8)
        columns = as_columns(rows8)
        kernel = kernel_block(columns, [rows8[axis : axis + 1] for axis in range(3)])
        row_sum = jnp.sum(kernel, axis=0, keepdims=True)
        row_scale = lax.rsqrt(gain[box : box + 1, :] * row_sum)
        column_scale = jnp.transpose(jnp.broadcast_to(row_scale, (8, NP)))[:, :1]
        residual = jnp.where(diagonal, 0.25, 0.0) - 0.75 * (column_scale * kernel * row_scale)
        r = pieces(residual)
        yield
        square = multiply(r, r)
        w = (32.0 / 31.0) * square - jnp.where(diagonal, 1.0 / 31.0, 0.0)
        wp = pieces(w)
        yield
        chosen = jnp.where(sub == pivots[box : box + 1, :], 1.0, 0.0).astype(BF16)
        loads[box][0].wait()
        lifted = pieces(chosen[:, :K].astype(F32) + select_right(chosen[:, K:], interp[box]))
        v = (961.0 * 2.0 / 1921.0) * multiply(wp, wp) - jnp.where(diagonal, 1.0 / 1921.0, 0.0)
        yield
        tail = w + v + multiply(wp, pieces(v))
        yield
        series = residual + tail + multiply(r, pieces(tail))
        factor = 0.75 * NP * (32.0 / 31.0) * (1922.0 / 1921.0)
        scaled = (factor * column_scale) * (series + jnp.where(diagonal, 1.0, 0.0)) * row_scale
        inverse[box] = scaled
        yield
        answer = multiply(pieces(scaled), lifted)
        response[box] = answer
        packed = select(rows8, chosen[:, :K], NN)
        for slot in range(NB):
            listed = neighbors[box, slot].astype(F32)
            packed = jnp.where((info_sub == 3) & (info_lane == slot), listed, packed)
        for panel in range(PANELS):
            message[panel, box, K:, :] = packed
        loads[box][1].wait()
        yield
        solved = multiply(pieces(answer), pieces(rhs[box]), TN)
        for panel in range(PANELS):
            message[panel, box, :K, :] = solved[:, panel * 128 : (panel + 1) * 128]
        yield

    for _ in zip(*[stages(box) for box in range(HERE)]):
        pass


def select_right(chosen, x):
    dot = lambda a: lax.dot_general(chosen, a, NT, preferred_element_type=F32)
    high = x.astype(BF16)
    rest = x - high.astype(F32)
    mid = rest.astype(BF16)
    low = (rest - mid.astype(F32)).astype(BF16)
    return dot(high) + (dot(mid) + dot(low))


VMEM = pl.BlockSpec(memory_space=pltpu.VMEM)
SMEM = pl.BlockSpec(memory_space=pltpu.SMEM)
HBM = pl.BlockSpec(memory_space=pltpu.HBM)


def near(*dims):
    return pltpu.VMEM(dims, F32)


def far_held(x):
    return pltpu.with_memory_space_constraint(x, pltpu.HBM)


def held(x):
    return pltpu.with_memory_space_constraint(x, pltpu.VMEM)


def factor_boxes(neighbors, points, gain, pivots, interp, rhs):
    return pl.pallas_call(
        factor_kernel,
        out_shape=(
            near(PANELS, HERE, ROWS, 128),
            near(HERE, NP, NP),
            near(HERE, NP, K),
            near(HERE, NP, COLS),
        ),
        in_specs=[SMEM] + [VMEM] * 3 + [HBM] * 2,
        out_specs=(VMEM,) * 4,
        scratch_shapes=[pltpu.VMEM((HERE, K, K), F32), pltpu.SemaphoreType.DMA((2, HERE))],
        compiler_params=GRANT,
        name="factor_boxes",
    )(neighbors, points, gain, pivots, far_held(interp), far_held(rhs))


def apply_kernel(inverse, rhs, start):
    for box in range(HERE):
        start[box] = multiply(pieces(inverse[box]), pieces(rhs[box]))


def apply_inverse(inverse, rhs):
    return pl.pallas_call(
        apply_kernel,
        out_shape=near(HERE, NP, COLS),
        in_specs=[VMEM] * 2,
        out_specs=VMEM,
        compiler_params=GRANT,
        name="apply_inverse",
    )(held(inverse), held(rhs))


def own_kernel(boxes, total, lists):
    lists[...] = jnp.concatenate([boxes[c, K + 3 : K + 4, :] for c in range(CHILD)], axis=0).astype(jnp.int32)
    values = pieces(jnp.concatenate([boxes[c, :K, :] * (1.0 / NP) for c in range(CHILD)], axis=0))
    for target in range(CHILD):
        columns = as_columns(boxes[target, K:, :])
        blocks = []
        for source in range(CHILD):
            if source == target:
                blocks.append(jnp.zeros((K, K), F32))
            else:
                rows = [boxes[source, K + axis : K + axis + 1, :] for axis in range(3)]
                blocks.append(kernel_block(columns, rows))
        total[target] = multiply(pieces(jnp.concatenate(blocks, axis=1)), values)


def own_terms(boxes):
    return pl.pallas_call(
        own_kernel,
        out_shape=(near(CHILD, K, 128), pltpu.VMEM((CHILD, 128), jnp.int32)),
        in_specs=[VMEM],
        out_specs=(VMEM,) * 2,
        compiler_params=GRANT,
        name="own_terms",
    )(held(boxes))


def listed_kernel(lists, boxes, own, inner, outer, total, high, low, places):
    even = (lax.axis_index("box") % 2) == 0
    for ref, base in ((inner, jnp.where(even, CHILD, 0)), (outer, jnp.where(even, 0, CHILD))):
        for source in range(CHILD):
            up, down = pieces(ref[source, :K, :] * (1.0 / NP))
            high[base + source] = up
            low[base + source] = down
            places[base + source] = ref[source, K:, :]
    for target in range(CHILD):
        columns = as_columns(boxes[target, K:, :])
        blocks, ups, downs = [], [], []
        for slot in range(NB):
            source = lists[target, slot]
            rows8 = places[source]
            blocks.append(kernel_block(columns, [rows8[axis : axis + 1] for axis in range(3)]))
            ups.append(high[source])
            downs.append(low[source])
        values = (jnp.concatenate(ups, axis=0), jnp.concatenate(downs, axis=0))
        total[target] = own[target] + multiply(pieces(jnp.concatenate(blocks, axis=1)), values)


def listed_terms(lists, boxes, own, inner, outer):
    return pl.pallas_call(
        listed_kernel,
        out_shape=near(CHILD, K, 128),
        in_specs=[SMEM] + [VMEM] * 4,
        out_specs=VMEM,
        scratch_shapes=[
            pltpu.VMEM((2 * CHILD, K, 128), BF16),
            pltpu.VMEM((2 * CHILD, K, 128), BF16),
            pltpu.VMEM((2 * CHILD, 8, 128), F32),
        ],
        compiler_params=GRANT,
        name="listed_terms",
    )(lists, held(boxes), held(own), held(inner), held(outer))


def finish_kernel(start, response, total, out, ready, sems):
    stores = []
    for box in range(HERE):
        factor = pieces(response[box])
        for half in range(2):
            cols = slice(half * (COLS // 2), (half + 1) * (COLS // 2))
            panels = [total[2 * half + panel, box] for panel in range(2)]
            correction = jnp.concatenate(panels, axis=1)
            ready[box, half] = start[box, :, cols] - multiply(factor, pieces(correction))
            store = pltpu.make_async_copy(
                ready.at[box, half], out.at[box, :, cols], sems.at[box, half]
            )
            store.start()
            stores.append(store)
    for store in stores:
        store.wait()


def finish_boxes(start, response, total):
    return pl.pallas_call(
        finish_kernel,
        out_shape=jax.ShapeDtypeStruct((HERE, NP, COLS), F32),
        in_specs=[VMEM] * 3,
        out_specs=HBM,
        scratch_shapes=[
            pltpu.VMEM((HERE, 2, NP, COLS // 2), F32),
            pltpu.SemaphoreType.DMA((HERE, 2)),
        ],
        compiler_params=GRANT,
        name="finish_boxes",
    )(held(start), held(response), held(total))


def exchanged(block, partner):
    groups = range(lax.axis_size("box"))
    return lax.ppermute(block, "box", [(i, partner(i)) for i in groups if partner(i) in groups])


def inner_partner(i):
    return i ^ 1


def outer_partner(i):
    return i - 1 if i % 2 == 0 else i + 1


def per_device(points, self_gain, pivots, interp, neighbors, rhs):
    message, inverse, response, rhs_near = factor_boxes(
        neighbors[0],
        jnp.transpose(points[0], (1, 0, 2)),
        self_gain[0],
        pivots[0],
        interp[0],
        rhs[0],
    )
    boxes = lax.all_to_all(message, "coarse", 0, 0, tiled=True).reshape(CHILD, ROWS, 128)
    outer = exchanged(boxes, outer_partner)
    inner = exchanged(boxes, inner_partner)
    own, lists = own_terms(boxes)
    start = apply_inverse(inverse, rhs_near)
    total = listed_terms(lists, boxes, own, inner, outer)
    total = lax.all_to_all(total.reshape(PANELS, HERE, K, 128), "coarse", 0, 0, tiled=True)
    return finish_boxes(start, response, total)[None]


def solution(mesh):
    in_specs = (
        P("box", "coarse", None, None),
        P("box", "coarse", None),
        P("box", "coarse", None),
        P("box", "coarse", None, None),
        P("box", "coarse", None),
        P("box", "coarse", None, None),
    )
    out_specs = P("box", "coarse", None, None)
    return jax.shard_map(
        per_device, mesh=mesh, in_specs=in_specs, out_specs=out_specs, check_vma=False
    )
```

```python
import jax
import jax.numpy as jnp
from jax import lax
from jax.experimental import pallas as pl
from jax.experimental.pallas import tpu as pltpu
from jax.sharding import PartitionSpec as P

NP = 256
K = 128
COLS = 512
CHILD = 8
NB = 6
HERE = 2
PANELS = COLS // 128
ROWS = K + 8
F32 = jnp.float32
BF16 = jnp.bfloat16

softening = 0.0025

GRANT = pltpu.CompilerParams(vmem_limit_bytes=16 * 2**20)

NN = (((1,), (0,)), ((), ()))
NT = (((1,), (1,)), ((), ()))
TN = (((0,), (0,)), ((), ()))


def pieces(x):
    high = x.astype(BF16)
    return high, (x - high.astype(F32)).astype(BF16)


def multiply(left, right, dims=NN):
    dot = lambda a, b: lax.dot_general(a, b, dims, preferred_element_type=F32)
    return dot(left[0], right[0]) + (dot(left[0], right[1]) + dot(left[1], right[0]))


def once(left, right):
    return lax.dot_general(left, right, NN, preferred_element_type=F32)


def select(x, chosen, dims):
    dot = lambda a: lax.dot_general(a, chosen, dims, preferred_element_type=F32)
    high = x.astype(BF16)
    rest = x - high.astype(F32)
    mid = rest.astype(BF16)
    low = (rest - mid.astype(F32)).astype(BF16)
    return dot(high) + (dot(mid) + dot(low))


def kernel_block(columns, rows):
    square = None
    for axis in range(3):
        difference = columns[axis] - rows[axis]
        square = difference * difference if square is None else square + difference * difference
    return lax.rsqrt(square + softening)


def as_columns(rows8):
    turned = jnp.transpose(rows8)
    return [turned[:, axis : axis + 1] for axis in range(3)]


def factor_kernel(
    neighbors, points, gain, pivots, interp_hbm, rhs_hbm,
    message, inverse, response, rhs, interp, sems,
):
    loads = [
        (
            pltpu.make_async_copy(interp_hbm.at[box], interp.at[box], sems.at[0, box]),
            pltpu.make_async_copy(rhs_hbm.at[box], rhs.at[box], sems.at[1, box]),
        )
        for box in range(HERE)
    ]
    for step in range(2):
        for box in range(HERE):
            loads[box][step].start()
    group = lax.axis_index("box")
    first_child = HERE * lax.axis_index("coarse")
    sub = lax.broadcasted_iota(jnp.int32, (NP, NP), 0)
    lane = lax.broadcasted_iota(jnp.int32, (NP, NP), 1)
    small_sub = lax.broadcasted_iota(jnp.int32, (8, NP), 0)
    info_sub = lax.broadcasted_iota(jnp.int32, (8, 128), 0)
    info_lane = lax.broadcasted_iota(jnp.int32, (8, 128), 1)
    diagonal = sub == lane

    def stages(box):
        child = first_child + box
        corner = (2 * group + child % 2, child // 2 % 2, child // 4)
        rows8 = jnp.zeros((8, NP), F32)
        for axis in range(3):
            coordinate = points[axis, box : box + 1, :] + corner[axis].astype(F32)
            rows8 = jnp.where(small_sub == axis, coordinate, rows8)
        columns = as_columns(rows8)
        kernel = kernel_block(columns, [rows8[axis : axis + 1] for axis in range(3)])
        row_sum = jnp.sum(kernel, axis=0, keepdims=True)
        row_scale = lax.rsqrt(gain[box : box + 1, :] * row_sum)
        column_scale = jnp.transpose(jnp.broadcast_to(row_scale, (8, NP)))[:, :1]
        residual = jnp.where(diagonal, 0.25, 0.0) - 0.75 * (column_scale * kernel * row_scale)
        r = pieces(residual)
        yield
        square = multiply(r, r)
        w = (32.0 / 31.0) * square - jnp.where(diagonal, 1.0 / 31.0, 0.0)
        wp = pieces(w)
        yield
        chosen = jnp.where(sub == pivots[box : box + 1, :], 1.0, 0.0).astype(BF16)
        loads[box][0].wait()
        lifted = pieces(chosen[:, :K].astype(F32) + select_right(chosen[:, K:], interp[box]))
        v = (961.0 * 2.0 / 1921.0) * once(wp[0], wp[0]) - jnp.where(diagonal, 1.0 / 1921.0, 0.0)
        yield
        tail = w + v + once(wp[0], v.astype(BF16))
        yield
        series = residual + tail + multiply(r, pieces(tail))
        factor = 0.75 * NP * (32.0 / 31.0) * (1922.0 / 1921.0)
        scaled = (factor * column_scale) * (series + jnp.where(diagonal, 1.0, 0.0)) * row_scale
        inverse[box] = scaled
        yield
        answer = multiply(pieces(scaled), lifted)
        response[box] = answer
        packed = select(rows8, chosen[:, :K], NN)
        for slot in range(NB):
            listed = neighbors[box, slot].astype(F32)
            packed = jnp.where((info_sub == 3) & (info_lane == slot), listed, packed)
        for panel in range(PANELS):
            message[panel, box, K:, :] = packed
        loads[box][1].wait()
        yield
        solved = multiply(pieces(answer), pieces(rhs[box]), TN)
        for panel in range(PANELS):
            message[panel, box, :K, :] = solved[:, panel * 128 : (panel + 1) * 128]
        yield

    for _ in zip(*[stages(box) for box in range(HERE)]):
        pass


def select_right(chosen, x):
    dot = lambda a: lax.dot_general(chosen, a, NT, preferred_element_type=F32)
    high = x.astype(BF16)
    rest = x - high.astype(F32)
    mid = rest.astype(BF16)
    low = (rest - mid.astype(F32)).astype(BF16)
    return dot(high) + (dot(mid) + dot(low))


VMEM = pl.BlockSpec(memory_space=pltpu.VMEM)
SMEM = pl.BlockSpec(memory_space=pltpu.SMEM)
HBM = pl.BlockSpec(memory_space=pltpu.HBM)


def near(*dims):
    return pltpu.VMEM(dims, F32)


def far_held(x):
    return pltpu.with_memory_space_constraint(x, pltpu.HBM)


def held(x):
    return pltpu.with_memory_space_constraint(x, pltpu.VMEM)


def factor_boxes(neighbors, points, gain, pivots, interp, rhs):
    return pl.pallas_call(
        factor_kernel,
        out_shape=(
            near(PANELS, HERE, ROWS, 128),
            near(HERE, NP, NP),
            near(HERE, NP, K),
            near(HERE, NP, COLS),
        ),
        in_specs=[SMEM] + [VMEM] * 3 + [HBM] * 2,
        out_specs=(VMEM,) * 4,
        scratch_shapes=[pltpu.VMEM((HERE, K, K), F32), pltpu.SemaphoreType.DMA((2, HERE))],
        compiler_params=GRANT,
        name="factor_boxes",
    )(neighbors, points, gain, pivots, far_held(interp), far_held(rhs))


def own_kernel(boxes, inverse, rhs, total, lists, start):
    lists[...] = jnp.concatenate([boxes[c, K + 3 : K + 4, :] for c in range(CHILD)], axis=0).astype(jnp.int32)
    values = pieces(jnp.concatenate([boxes[c, :K, :] * (1.0 / NP) for c in range(CHILD)], axis=0))
    for target in range(CHILD):
        columns = as_columns(boxes[target, K:, :])
        blocks = []
        for source in range(CHILD):
            if source == target:
                blocks.append(jnp.zeros((K, K), F32))
            else:
                rows = [boxes[source, K + axis : K + axis + 1, :] for axis in range(3)]
                blocks.append(kernel_block(columns, rows))
        total[target] = multiply(pieces(jnp.concatenate(blocks, axis=1)), values)
    for box in range(HERE):
        start[box] = multiply(pieces(inverse[box]), pieces(rhs[box]))


def own_terms(boxes, inverse, rhs):
    return pl.pallas_call(
        own_kernel,
        out_shape=(
            near(CHILD, K, 128),
            pltpu.VMEM((CHILD, 128), jnp.int32),
            near(HERE, NP, COLS),
        ),
        in_specs=[VMEM] * 3,
        out_specs=(VMEM,) * 3,
        compiler_params=GRANT,
        name="own_terms",
    )(held(boxes), held(inverse), held(rhs))


def listed_kernel(
    lists_near, boxes, own, inner, outer, total, high, low, places, lists, sem
):
    load = pltpu.make_async_copy(lists_near, lists, sem)
    load.start()
    even = (lax.axis_index("box") % 2) == 0
    for ref, base in ((inner, jnp.where(even, CHILD, 0)), (outer, jnp.where(even, 0, CHILD))):
        for source in range(CHILD):
            up, down = pieces(ref[source, :K, :] * (1.0 / NP))
            high[base + source] = up
            low[base + source] = down
            places[base + source] = ref[source, K:, :]
    load.wait()
    for target in range(CHILD):
        columns = as_columns(boxes[target, K:, :])
        blocks, ups, downs = [], [], []
        for slot in range(NB):
            source = lists[target, slot]
            rows8 = places[source]
            blocks.append(kernel_block(columns, [rows8[axis : axis + 1] for axis in range(3)]))
            ups.append(high[source])
            downs.append(low[source])
        values = (jnp.concatenate(ups, axis=0), jnp.concatenate(downs, axis=0))
        total[target] = own[target] + multiply(pieces(jnp.concatenate(blocks, axis=1)), values)


def listed_terms(lists, boxes, own, inner, outer):
    return pl.pallas_call(
        listed_kernel,
        out_shape=near(CHILD, K, 128),
        in_specs=[VMEM] * 5,
        out_specs=VMEM,
        scratch_shapes=[
            pltpu.VMEM((2 * CHILD, K, 128), BF16),
            pltpu.VMEM((2 * CHILD, K, 128), BF16),
            pltpu.VMEM((2 * CHILD, 8, 128), F32),
            pltpu.SMEM((CHILD, 128), jnp.int32),
            pltpu.SemaphoreType.DMA,
        ],
        compiler_params=GRANT,
        name="listed_terms",
    )(held(lists), held(boxes), held(own), held(inner), held(outer))


def finish_kernel(start, response, total, out, ready, sems):
    stores = []
    for box in range(HERE):
        factor = pieces(response[box])
        for half in range(2):
            cols = slice(half * (COLS // 2), (half + 1) * (COLS // 2))
            panels = [total[2 * half + panel, box] for panel in range(2)]
            correction = jnp.concatenate(panels, axis=1)
            ready[box, half] = start[box, :, cols] - multiply(factor, pieces(correction))
            store = pltpu.make_async_copy(
                ready.at[box, half], out.at[box, :, cols], sems.at[box, half]
            )
            store.start()
            stores.append(store)
    for store in stores:
        store.wait()


def finish_boxes(start, response, total):
    return pl.pallas_call(
        finish_kernel,
        out_shape=jax.ShapeDtypeStruct((HERE, NP, COLS), F32),
        in_specs=[VMEM] * 3,
        out_specs=HBM,
        scratch_shapes=[
            pltpu.VMEM((HERE, 2, NP, COLS // 2), F32),
            pltpu.SemaphoreType.DMA((HERE, 2)),
        ],
        compiler_params=GRANT,
        name="finish_boxes",
    )(held(start), held(response), held(total))


def exchanged(block, partner):
    groups = range(lax.axis_size("box"))
    return lax.ppermute(block, "box", [(i, partner(i)) for i in groups if partner(i) in groups])


def inner_partner(i):
    return i ^ 1


def outer_partner(i):
    return i - 1 if i % 2 == 0 else i + 1


def per_device(points, self_gain, pivots, interp, neighbors, rhs):
    message, inverse, response, rhs_near = factor_boxes(
        neighbors[0],
        jnp.transpose(points[0], (1, 0, 2)),
        self_gain[0],
        pivots[0],
        interp[0],
        rhs[0],
    )
    boxes = lax.all_to_all(message, "coarse", 0, 0, tiled=True).reshape(CHILD, ROWS, 128)
    outer = exchanged(boxes, outer_partner)
    inner = exchanged(boxes, inner_partner)
    own, lists, start = own_terms(boxes, inverse, rhs_near)
    total = listed_terms(lists, boxes, own, inner, outer)
    total = lax.all_to_all(total.reshape(PANELS, HERE, K, 128), "coarse", 0, 0, tiled=True)
    return finish_boxes(start, response, total)[None]


def solution(mesh):
    in_specs = (
        P("box", "coarse", None, None),
        P("box", "coarse", None),
        P("box", "coarse", None),
        P("box", "coarse", None, None),
        P("box", "coarse", None),
        P("box", "coarse", None, None),
    )
    out_specs = P("box", "coarse", None, None)
    return jax.shard_map(
        per_device, mesh=mesh, in_specs=in_specs, out_specs=out_specs, check_vma=False
    )
```

```python
import jax
import jax.numpy as jnp
from jax import lax
from jax.experimental import pallas as pl
from jax.experimental.pallas import tpu as pltpu
from jax.sharding import PartitionSpec as P

NP = 256
K = 128
COLS = 512
CHILD = 8
NB = 6
HERE = 2
PANELS = COLS // 128
ROWS = HERE * K + 8
SCALE = 0.75 * NP * (32.0 / 31.0) * (1922.0 / 1921.0)
F32 = jnp.float32
BF16 = jnp.bfloat16

softening = 0.0025

GRANT = pltpu.CompilerParams(vmem_limit_bytes=16 * 2**20)

NN = (((1,), (0,)), ((), ()))
NT = (((1,), (1,)), ((), ()))
TN = (((0,), (0,)), ((), ()))


def pieces(x):
    high = x.astype(BF16)
    return high, (x - high.astype(F32)).astype(BF16)


def multiply(left, right, dims=NN):
    dot = lambda a, b: lax.dot_general(a, b, dims, preferred_element_type=F32)
    return dot(left[0], right[0]) + (dot(left[0], right[1]) + dot(left[1], right[0]))


def once(left, right):
    return lax.dot_general(left, right, NN, preferred_element_type=F32)


def third_factor(wp, diagonal):
    return (961.0 * 2.0 / 1921.0) * once(wp[0], wp[0]) - jnp.where(diagonal, 1.0 / 1921.0, 0.0)


def select(x, chosen, dims):
    dot = lambda a: lax.dot_general(a, chosen, dims, preferred_element_type=F32)
    high = x.astype(BF16)
    rest = x - high.astype(F32)
    mid = rest.astype(BF16)
    low = (rest - mid.astype(F32)).astype(BF16)
    return dot(high) + (dot(mid) + dot(low))


def kernel_block(columns, rows):
    square = None
    for axis in range(3):
        difference = columns[axis] - rows[axis]
        square = difference * difference if square is None else square + difference * difference
    return lax.rsqrt(square + softening)


def as_columns(rows8):
    turned = jnp.transpose(rows8)
    return [turned[:, axis : axis + 1] for axis in range(3)]


def factor_kernel(
    neighbors, points, gain, pivots, interp_hbm, rhs_hbm,
    message, residuals, seconds, scales, response, rhs, interp, sems,
):
    loads = [
        (
            pltpu.make_async_copy(interp_hbm.at[box], interp.at[box], sems.at[0, box]),
            pltpu.make_async_copy(rhs_hbm.at[box], rhs.at[box], sems.at[1, box]),
        )
        for box in range(HERE)
    ]
    for step in range(2):
        for box in range(HERE):
            loads[box][step].start()
    group = lax.axis_index("box")
    first_child = HERE * lax.axis_index("coarse")
    sub = lax.broadcasted_iota(jnp.int32, (NP, NP), 0)
    lane = lax.broadcasted_iota(jnp.int32, (NP, NP), 1)
    small_sub = lax.broadcasted_iota(jnp.int32, (8, NP), 0)
    info_sub = lax.broadcasted_iota(jnp.int32, (8, 128), 0)
    info_lane = lax.broadcasted_iota(jnp.int32, (8, 128), 1)
    diagonal = sub == lane

    def stages(box):
        child = first_child + box
        corner = (2 * group + child % 2, child // 2 % 2, child // 4)
        rows8 = jnp.zeros((8, NP), F32)
        for axis in range(3):
            coordinate = points[axis, box : box + 1, :] + corner[axis].astype(F32)
            rows8 = jnp.where(small_sub == axis, coordinate, rows8)
        columns = as_columns(rows8)
        kernel = kernel_block(columns, [rows8[axis : axis + 1] for axis in range(3)])
        row_sum = jnp.sum(kernel, axis=0, keepdims=True)
        row_scale = lax.rsqrt(gain[box : box + 1, :] * row_sum)
        column_scale = jnp.transpose(jnp.broadcast_to(row_scale, (8, NP)))[:, :1]
        residual = jnp.where(diagonal, 0.25, 0.0) - 0.75 * (column_scale * kernel * row_scale)
        r = pieces(residual)
        yield
        square = multiply(r, r)
        w = (32.0 / 31.0) * square - jnp.where(diagonal, 1.0 / 31.0, 0.0)
        wp = pieces(w)
        yield
        residuals[box] = residual
        seconds[box] = w
        scales[box] = jnp.broadcast_to(row_scale, (8, NP))
        chosen = jnp.where(sub == pivots[box : box + 1, :], 1.0, 0.0).astype(BF16)
        loads[box][0].wait()
        loads[box][1].wait()
        right = pieces(rhs[box])
        lifted = chosen[:, :K].astype(F32) + select_right(chosen[:, K:], interp[box])
        third = third_factor(wp, diagonal)
        answer = column_scale * lifted
        yield
        answer = answer + once(third.astype(BF16), answer.astype(BF16))
        yield
        answer = answer + multiply(wp, pieces(answer))
        yield
        answer = (SCALE * column_scale) * (answer + multiply(r, pieces(answer)))
        response[box] = answer
        packed = select(rows8, chosen[:, :K], NN)
        for slot in range(NB):
            listed = neighbors[box, slot].astype(F32)
            packed = jnp.where((info_sub == 3) & (info_lane == slot), listed, packed)
        for panel in range(PANELS):
            message[panel, HERE * K + 4 * box : HERE * K + 4 * box + 4, :] = packed[:4]
        yield
        solved = multiply(pieces(answer), right, TN)
        for panel in range(PANELS):
            columns_here = slice(panel * 128, (panel + 1) * 128)
            message[panel, box * K : (box + 1) * K, :] = solved[:, columns_here]
        yield

    for _ in zip(*[stages(box) for box in range(HERE)]):
        pass


def select_right(chosen, x):
    dot = lambda a: lax.dot_general(chosen, a, NT, preferred_element_type=F32)
    high = x.astype(BF16)
    rest = x - high.astype(F32)
    mid = rest.astype(BF16)
    low = (rest - mid.astype(F32)).astype(BF16)
    return dot(high) + (dot(mid) + dot(low))


VMEM = pl.BlockSpec(memory_space=pltpu.VMEM)
SMEM = pl.BlockSpec(memory_space=pltpu.SMEM)
HBM = pl.BlockSpec(memory_space=pltpu.HBM)


def near(*dims):
    return pltpu.VMEM(dims, F32)


def far_held(x):
    return pltpu.with_memory_space_constraint(x, pltpu.HBM)


def held(x):
    return pltpu.with_memory_space_constraint(x, pltpu.VMEM)


def factor_boxes(neighbors, points, gain, pivots, interp, rhs):
    return pl.pallas_call(
        factor_kernel,
        out_shape=(
            near(PANELS, ROWS, 128),
            near(HERE, NP, NP),
            near(HERE, NP, NP),
            near(HERE, 8, NP),
            near(HERE, NP, K),
            near(HERE, NP, COLS),
        ),
        in_specs=[SMEM] + [VMEM] * 3 + [HBM] * 2,
        out_specs=(VMEM,) * 6,
        scratch_shapes=[pltpu.VMEM((HERE, K, K), F32), pltpu.SemaphoreType.DMA((2, HERE))],
        compiler_params=GRANT,
        name="factor_boxes",
    )(neighbors, points, gain, pivots, far_held(interp), far_held(rhs))


def solves(ref, child):
    return ref[child // HERE, child % HERE * K : (child % HERE + 1) * K, :]


def info_row(ref, child, row):
    at = HERE * K + 4 * (child % HERE) + row
    return ref[child // HERE, at : at + 1, :]


def target_columns(ref):
    found = []
    for place in range(PANELS):
        turned = jnp.transpose(ref[place, HERE * K :, :])
        for box in range(HERE):
            found.append([turned[:, 4 * box + axis : 4 * box + axis + 1] for axis in range(3)])
    return found


def own_kernel(boxes, residuals, seconds, scales, rhs, total, lists, start):
    for c in range(CHILD):
        lists[c : c + 1, :] = info_row(boxes, c, 3).astype(jnp.int32)
    stacked = jnp.concatenate([solves(boxes, c) * (1.0 / NP) for c in range(CHILD)], axis=0)
    values = pieces(stacked)
    for target, columns in enumerate(target_columns(boxes)):
        blocks = []
        for source in range(CHILD):
            if source == target:
                blocks.append(jnp.zeros((K, K), F32))
            else:
                blocks.append(
                    kernel_block(columns, [info_row(boxes, source, axis) for axis in range(3)])
                )
        total[target] = multiply(pieces(jnp.concatenate(blocks, axis=1)), values)
    sub = lax.broadcasted_iota(jnp.int32, (NP, NP), 0)
    diagonal = sub == lax.broadcasted_iota(jnp.int32, (NP, NP), 1)

    def stages(box):
        residual, w = residuals[box], seconds[box]
        row_scale = scales[box, :1, :]
        column_scale = jnp.transpose(scales[box])[:, :1]
        wp = pieces(w)
        v = third_factor(wp, diagonal)
        yield
        tail = w + v + once(wp[0], v.astype(BF16))
        yield
        series = residual + tail + multiply(pieces(residual), pieces(tail))
        inverse = (SCALE * column_scale) * (series + jnp.where(diagonal, 1.0, 0.0)) * row_scale
        yield
        start[box] = multiply(pieces(inverse), pieces(rhs[box]))
        yield

    for _ in zip(*[stages(box) for box in range(HERE)]):
        pass


def own_terms(boxes, residuals, seconds, scales, rhs):
    return pl.pallas_call(
        own_kernel,
        out_shape=(
            near(CHILD, K, 128),
            pltpu.VMEM((CHILD, 128), jnp.int32),
            near(HERE, NP, COLS),
        ),
        in_specs=[VMEM] * 5,
        out_specs=(VMEM,) * 3,
        compiler_params=GRANT,
        name="own_terms",
    )(held(boxes), held(residuals), held(seconds), held(scales), held(rhs))


def listed_kernel(
    lists_near, boxes, own, inner, outer, total, high, low, places, lists, sem
):
    load = pltpu.make_async_copy(lists_near, lists, sem)
    load.start()
    even = (lax.axis_index("box") % 2) == 0
    for ref, base in ((inner, jnp.where(even, CHILD, 0)), (outer, jnp.where(even, 0, CHILD))):
        for source in range(CHILD):
            up, down = pieces(solves(ref, source) * (1.0 / NP))
            high[base + source] = up
            low[base + source] = down
            for axis in range(3):
                places[base + source, axis : axis + 1, :] = info_row(ref, source, axis)
    load.wait()
    for target, columns in enumerate(target_columns(boxes)):
        blocks, ups, downs = [], [], []
        for slot in range(NB):
            source = lists[target, slot]
            rows = [places[source, axis : axis + 1, :] for axis in range(3)]
            blocks.append(kernel_block(columns, rows))
            ups.append(high[source])
            downs.append(low[source])
        values = (jnp.concatenate(ups, axis=0), jnp.concatenate(downs, axis=0))
        total[target] = own[target] + multiply(pieces(jnp.concatenate(blocks, axis=1)), values)


def listed_terms(lists, boxes, own, inner, outer):
    return pl.pallas_call(
        listed_kernel,
        out_shape=near(CHILD, K, 128),
        in_specs=[VMEM] * 5,
        out_specs=VMEM,
        scratch_shapes=[
            pltpu.VMEM((2 * CHILD, K, 128), BF16),
            pltpu.VMEM((2 * CHILD, K, 128), BF16),
            pltpu.VMEM((2 * CHILD, 8, 128), F32),
            pltpu.SMEM((CHILD, 128), jnp.int32),
            pltpu.SemaphoreType.DMA,
        ],
        compiler_params=GRANT,
        name="listed_terms",
    )(held(lists), held(boxes), held(own), held(inner), held(outer))


def finish_kernel(start, response, total, out, ready, sems):
    stores = []
    for box in range(HERE):
        factor = pieces(response[box])
        for half in range(2):
            cols = slice(half * (COLS // 2), (half + 1) * (COLS // 2))
            panels = [total[2 * half + panel, box] for panel in range(2)]
            correction = jnp.concatenate(panels, axis=1)
            ready[box, half] = start[box, :, cols] - multiply(factor, pieces(correction))
            store = pltpu.make_async_copy(
                ready.at[box, half], out.at[box, :, cols], sems.at[box, half]
            )
            store.start()
            stores.append(store)
    for store in stores:
        store.wait()


def finish_boxes(start, response, total):
    return pl.pallas_call(
        finish_kernel,
        out_shape=jax.ShapeDtypeStruct((HERE, NP, COLS), F32),
        in_specs=[VMEM] * 3,
        out_specs=HBM,
        scratch_shapes=[
            pltpu.VMEM((HERE, 2, NP, COLS // 2), F32),
            pltpu.SemaphoreType.DMA((HERE, 2)),
        ],
        compiler_params=GRANT,
        name="finish_boxes",
    )(held(start), held(response), held(total))


def exchanged(block, partner):
    groups = range(lax.axis_size("box"))
    return lax.ppermute(block, "box", [(i, partner(i)) for i in groups if partner(i) in groups])


def inner_partner(i):
    return i ^ 1


def outer_partner(i):
    return i - 1 if i % 2 == 0 else i + 1


def per_device(points, self_gain, pivots, interp, neighbors, rhs):
    message, residuals, seconds, scales, response, rhs_near = factor_boxes(
        neighbors[0],
        jnp.transpose(points[0], (1, 0, 2)),
        self_gain[0],
        pivots[0],
        interp[0],
        rhs[0],
    )
    boxes = lax.all_to_all(message, "coarse", 0, 0, tiled=True)
    outer = exchanged(boxes, outer_partner)
    inner = exchanged(boxes, inner_partner)
    own, lists, start = own_terms(boxes, residuals, seconds, scales, rhs_near)
    total = listed_terms(lists, boxes, own, inner, outer)
    total = lax.all_to_all(total.reshape(PANELS, HERE, K, 128), "coarse", 0, 0, tiled=True)
    return finish_boxes(start, response, total)[None]


def solution(mesh):
    in_specs = (
        P("box", "coarse", None, None),
        P("box", "coarse", None),
        P("box", "coarse", None),
        P("box", "coarse", None, None),
        P("box", "coarse", None),
        P("box", "coarse", None, None),
    )
    out_specs = P("box", "coarse", None, None)
    return jax.shard_map(
        per_device, mesh=mesh, in_specs=in_specs, out_specs=out_specs, check_vma=False
    )
```

```python
import jax
import jax.numpy as jnp
from jax import lax
from jax.experimental import pallas as pl
from jax.experimental.pallas import tpu as pltpu
from jax.sharding import PartitionSpec as P

NP = 256
K = 128
COLS = 512
CHILD = 8
NB = 6
HERE = 2
PANELS = COLS // 128
ROWS = HERE * K + 8
SCALE = 0.75 * NP * (32.0 / 31.0) * (1922.0 / 1921.0)
F32 = jnp.float32
BF16 = jnp.bfloat16

softening = 0.0025

GRANT = pltpu.CompilerParams(vmem_limit_bytes=16 * 2**20)

NN = (((1,), (0,)), ((), ()))
NT = (((1,), (1,)), ((), ()))
TN = (((0,), (0,)), ((), ()))


def pieces(x):
    high = x.astype(BF16)
    return high, (x - high.astype(F32)).astype(BF16)


def multiply(left, right, dims=NN):
    dot = lambda a, b: lax.dot_general(a, b, dims, preferred_element_type=F32)
    return dot(left[0], right[0]) + (dot(left[0], right[1]) + dot(left[1], right[0]))


def once(left, right):
    return lax.dot_general(left, right, NN, preferred_element_type=F32)


def third_factor(wp, diagonal):
    return (961.0 * 2.0 / 1921.0) * once(wp[0], wp[0]) - jnp.where(diagonal, 1.0 / 1921.0, 0.0)


def select(x, chosen, dims):
    dot = lambda a: lax.dot_general(a, chosen, dims, preferred_element_type=F32)
    high = x.astype(BF16)
    rest = x - high.astype(F32)
    mid = rest.astype(BF16)
    low = (rest - mid.astype(F32)).astype(BF16)
    return dot(high) + (dot(mid) + dot(low))


def kernel_block(columns, rows):
    square = None
    for axis in range(3):
        difference = columns[axis] - rows[axis]
        square = difference * difference if square is None else square + difference * difference
    return lax.rsqrt(square + softening)


def as_columns(rows8):
    turned = jnp.transpose(rows8)
    return [turned[:, axis : axis + 1] for axis in range(3)]


def factor_kernel(
    neighbors, points, gain, pivots, interp_hbm, rhs_hbm,
    message, residuals, seconds, scales, response, rhs, interp, sems,
):
    loads = [
        (
            pltpu.make_async_copy(interp_hbm.at[box], interp.at[box], sems.at[0, box]),
            pltpu.make_async_copy(rhs_hbm.at[box], rhs.at[box], sems.at[1, box]),
        )
        for box in range(HERE)
    ]
    for step in range(2):
        for box in range(HERE):
            loads[box][step].start()
    group = lax.axis_index("box")
    first_child = HERE * lax.axis_index("coarse")
    sub = lax.broadcasted_iota(jnp.int32, (NP, NP), 0)
    lane = lax.broadcasted_iota(jnp.int32, (NP, NP), 1)
    small_sub = lax.broadcasted_iota(jnp.int32, (8, NP), 0)
    info_sub = lax.broadcasted_iota(jnp.int32, (8, 128), 0)
    info_lane = lax.broadcasted_iota(jnp.int32, (8, 128), 1)
    diagonal = sub == lane

    def stages(box):
        child = first_child + box
        corner = (2 * group + child % 2, child // 2 % 2, child // 4)
        rows8 = jnp.zeros((8, NP), F32)
        for axis in range(3):
            coordinate = points[axis, box : box + 1, :] + corner[axis].astype(F32)
            rows8 = jnp.where(small_sub == axis, coordinate, rows8)
        columns = as_columns(rows8)
        kernel = kernel_block(columns, [rows8[axis : axis + 1] for axis in range(3)])
        row_sum = jnp.sum(kernel, axis=0, keepdims=True)
        row_scale = lax.rsqrt(gain[box : box + 1, :] * row_sum)
        column_scale = jnp.transpose(jnp.broadcast_to(row_scale, (8, NP)))[:, :1]
        residual = jnp.where(diagonal, 0.25, 0.0) - 0.75 * (column_scale * kernel * row_scale)
        r = pieces(residual)
        yield
        square = multiply(r, r)
        w = (32.0 / 31.0) * square - jnp.where(diagonal, 1.0 / 31.0, 0.0)
        wp = pieces(w)
        yield
        residuals[box] = residual
        seconds[box] = w
        scales[box] = jnp.broadcast_to(row_scale, (8, NP))
        chosen = jnp.where(sub == pivots[box : box + 1, :], 1.0, 0.0).astype(BF16)
        loads[box][0].wait()
        loads[box][1].wait()
        right = pieces(rhs[box])
        lifted = chosen[:, :K].astype(F32) + select_right(chosen[:, K:], interp[box])
        third = third_factor(wp, diagonal)
        answer = column_scale * lifted
        yield
        answer = answer + once(third.astype(BF16), answer.astype(BF16))
        yield
        answer = answer + multiply(wp, pieces(answer))
        yield
        answer = (SCALE * column_scale) * (answer + multiply(r, pieces(answer)))
        response[box] = answer
        packed = select(rows8, chosen[:, :K], NN)
        for slot in range(NB):
            listed = neighbors[box, slot].astype(F32)
            packed = jnp.where((info_sub == 3) & (info_lane == slot), listed, packed)
        for panel in range(PANELS):
            message[panel, HERE * K + 4 * box : HERE * K + 4 * box + 4, :] = packed[:4]
        yield
        solved = multiply(pieces(answer), right, TN)
        for panel in range(PANELS):
            columns_here = slice(panel * 128, (panel + 1) * 128)
            message[panel, box * K : (box + 1) * K, :] = solved[:, columns_here]
        yield

    for _ in zip(*[stages(box) for box in range(HERE)]):
        pass


def select_right(chosen, x):
    dot = lambda a: lax.dot_general(chosen, a, NT, preferred_element_type=F32)
    high = x.astype(BF16)
    rest = x - high.astype(F32)
    mid = rest.astype(BF16)
    low = (rest - mid.astype(F32)).astype(BF16)
    return dot(high) + (dot(mid) + dot(low))


VMEM = pl.BlockSpec(memory_space=pltpu.VMEM)
SMEM = pl.BlockSpec(memory_space=pltpu.SMEM)
HBM = pl.BlockSpec(memory_space=pltpu.HBM)


def near(*dims):
    return pltpu.VMEM(dims, F32)


def far_held(x):
    return pltpu.with_memory_space_constraint(x, pltpu.HBM)


def held(x):
    return pltpu.with_memory_space_constraint(x, pltpu.VMEM)


def factor_boxes(neighbors, points, gain, pivots, interp, rhs):
    return pl.pallas_call(
        factor_kernel,
        out_shape=(
            near(PANELS, ROWS, 128),
            near(HERE, NP, NP),
            near(HERE, NP, NP),
            near(HERE, 8, NP),
            near(HERE, NP, K),
            near(HERE, NP, COLS),
        ),
        in_specs=[SMEM] + [VMEM] * 3 + [HBM] * 2,
        out_specs=(VMEM,) * 6,
        scratch_shapes=[pltpu.VMEM((HERE, K, K), F32), pltpu.SemaphoreType.DMA((2, HERE))],
        compiler_params=GRANT,
        name="factor_boxes",
    )(*[far_held(x) for x in (neighbors, points, gain, pivots, interp, rhs)])


def solves(ref, child):
    return ref[child // HERE, child % HERE * K : (child % HERE + 1) * K, :]


def info_row(ref, child, row):
    at = HERE * K + 4 * (child % HERE) + row
    return ref[child // HERE, at : at + 1, :]


def target_columns(ref):
    found = []
    for place in range(PANELS):
        turned = jnp.transpose(ref[place, HERE * K :, :])
        for box in range(HERE):
            found.append([turned[:, 4 * box + axis : 4 * box + axis + 1] for axis in range(3)])
    return found


def own_kernel(boxes, residuals, seconds, scales, rhs, total, lists, start):
    for c in range(CHILD):
        lists[c : c + 1, :] = info_row(boxes, c, 3).astype(jnp.int32)
    stacked = jnp.concatenate([solves(boxes, c) * (1.0 / NP) for c in range(CHILD)], axis=0)
    values = pieces(stacked)
    for target, columns in enumerate(target_columns(boxes)):
        blocks = []
        for source in range(CHILD):
            if source == target:
                blocks.append(jnp.zeros((K, K), F32))
            else:
                blocks.append(
                    kernel_block(columns, [info_row(boxes, source, axis) for axis in range(3)])
                )
        total[target] = multiply(pieces(jnp.concatenate(blocks, axis=1)), values)
    sub = lax.broadcasted_iota(jnp.int32, (NP, NP), 0)
    diagonal = sub == lax.broadcasted_iota(jnp.int32, (NP, NP), 1)

    def stages(box):
        residual, w = residuals[box], seconds[box]
        row_scale = scales[box, :1, :]
        column_scale = jnp.transpose(scales[box])[:, :1]
        wp = pieces(w)
        v = third_factor(wp, diagonal)
        yield
        tail = w + v + once(wp[0], v.astype(BF16))
        yield
        series = residual + tail + multiply(pieces(residual), pieces(tail))
        inverse = (SCALE * column_scale) * (series + jnp.where(diagonal, 1.0, 0.0)) * row_scale
        yield
        start[box] = multiply(pieces(inverse), pieces(rhs[box]))
        yield

    for _ in zip(*[stages(box) for box in range(HERE)]):
        pass


def own_terms(boxes, residuals, seconds, scales, rhs):
    return pl.pallas_call(
        own_kernel,
        out_shape=(
            near(CHILD, K, 128),
            pltpu.VMEM((CHILD, 128), jnp.int32),
            near(HERE, NP, COLS),
        ),
        in_specs=[VMEM] * 5,
        out_specs=(VMEM,) * 3,
        compiler_params=GRANT,
        name="own_terms",
    )(held(boxes), held(residuals), held(seconds), held(scales), held(rhs))


def listed_kernel(
    lists_near, boxes, own, inner, outer, total, high, low, places, lists, sem
):
    load = pltpu.make_async_copy(lists_near, lists, sem)
    load.start()
    even = (lax.axis_index("box") % 2) == 0
    for ref, base in ((inner, jnp.where(even, CHILD, 0)), (outer, jnp.where(even, 0, CHILD))):
        for source in range(CHILD):
            up, down = pieces(solves(ref, source) * (1.0 / NP))
            high[base + source] = up
            low[base + source] = down
            for axis in range(3):
                places[base + source, axis : axis + 1, :] = info_row(ref, source, axis)
    load.wait()
    for target, columns in enumerate(target_columns(boxes)):
        blocks, ups, downs = [], [], []
        for slot in range(NB):
            source = lists[target, slot]
            rows = [places[source, axis : axis + 1, :] for axis in range(3)]
            blocks.append(kernel_block(columns, rows))
            ups.append(high[source])
            downs.append(low[source])
        values = (jnp.concatenate(ups, axis=0), jnp.concatenate(downs, axis=0))
        total[target] = own[target] + multiply(pieces(jnp.concatenate(blocks, axis=1)), values)


def listed_terms(lists, boxes, own, inner, outer):
    return pl.pallas_call(
        listed_kernel,
        out_shape=near(CHILD, K, 128),
        in_specs=[VMEM] * 5,
        out_specs=VMEM,
        scratch_shapes=[
            pltpu.VMEM((2 * CHILD, K, 128), BF16),
            pltpu.VMEM((2 * CHILD, K, 128), BF16),
            pltpu.VMEM((2 * CHILD, 8, 128), F32),
            pltpu.SMEM((CHILD, 128), jnp.int32),
            pltpu.SemaphoreType.DMA,
        ],
        compiler_params=GRANT,
        name="listed_terms",
    )(held(lists), held(boxes), held(own), held(inner), held(outer))


def finish_kernel(start, response, total, out, ready, sems):
    stores = []
    for box in range(HERE):
        factor = pieces(response[box])
        for half in range(2):
            cols = slice(half * (COLS // 2), (half + 1) * (COLS // 2))
            panels = [total[2 * half + panel, box] for panel in range(2)]
            correction = jnp.concatenate(panels, axis=1)
            ready[box, half] = start[box, :, cols] - multiply(factor, pieces(correction))
            store = pltpu.make_async_copy(
                ready.at[box, half], out.at[box, :, cols], sems.at[box, half]
            )
            store.start()
            stores.append(store)
    for store in stores:
        store.wait()


def finish_boxes(start, response, total):
    return pl.pallas_call(
        finish_kernel,
        out_shape=jax.ShapeDtypeStruct((HERE, NP, COLS), F32),
        in_specs=[VMEM] * 3,
        out_specs=HBM,
        scratch_shapes=[
            pltpu.VMEM((HERE, 2, NP, COLS // 2), F32),
            pltpu.SemaphoreType.DMA((HERE, 2)),
        ],
        compiler_params=GRANT,
        name="finish_boxes",
    )(held(start), held(response), held(total))


def exchanged(block, partner):
    groups = range(lax.axis_size("box"))
    return lax.ppermute(block, "box", [(i, partner(i)) for i in groups if partner(i) in groups])


def inner_partner(i):
    return i ^ 1


def outer_partner(i):
    return i - 1 if i % 2 == 0 else i + 1


def per_device(points, self_gain, pivots, interp, neighbors, rhs):
    message, residuals, seconds, scales, response, rhs_near = factor_boxes(
        neighbors[0],
        jnp.transpose(points[0], (1, 0, 2)),
        self_gain[0],
        pivots[0],
        interp[0],
        rhs[0],
    )
    boxes = lax.all_to_all(message, "coarse", 0, 0, tiled=True)
    outer = exchanged(boxes, outer_partner)
    inner = exchanged(boxes, inner_partner)
    own, lists, start = own_terms(boxes, residuals, seconds, scales, rhs_near)
    total = listed_terms(lists, boxes, own, inner, outer)
    total = lax.all_to_all(total.reshape(PANELS, HERE, K, 128), "coarse", 0, 0, tiled=True)
    return finish_boxes(start, response, total)[None]


def solution(mesh):
    in_specs = (
        P("box", "coarse", None, None),
        P("box", "coarse", None),
        P("box", "coarse", None),
        P("box", "coarse", None, None),
        P("box", "coarse", None),
        P("box", "coarse", None, None),
    )
    out_specs = P("box", "coarse", None, None)
    return jax.shard_map(
        per_device, mesh=mesh, in_specs=in_specs, out_specs=out_specs, check_vma=False
    )
```
